32 devices in a mesh: groups: 2 (over y), lon: 4 (over z), lat: 2 (over x), segment: 2 (over core).
Axes of the slice: x: 2, y: 2, z: 4, core: 2. Of those that a mesh axis runs over, the one named last changes fastest.
Arguments:
- inputs: bfloat16 [32, 128, 512], P(('groups', 'lat'), 'lon'), parts along dimension 0, may hold values from -6 to 6
- cotangent: bfloat16 [32, 128, 512], P(('groups', 'lat'), 'lon'), parts along dimension 0, may hold values from -8 to 8
- kernel: bfloat16 [2, 49, 512], P('segment'), may hold values from -0.875 to 0.875
- conv_bias: float32 [2, 512], P('segment'), may hold values from -3 to 3
- norm_gain: float32 [2, 512], P('segment'), may hold values from 0.5 to 2
- norm_shift: float32 [2, 512], P('segment'), may hold values from -3 to 3
- up_weight: bfloat16 [2, 512, 2048], P('segment'), may hold values from -0.25 to 0.25
- hidden_bias: float32 [2, 2048], P('segment'), may hold values from -3 to 3
- down_weight: bfloat16 [2, 2048, 512], P('segment'), may hold values from -0.125 to 0.125
- out_bias: float32 [2, 512], P('segment'), may hold values from -3 to 3
- layer_scale: float32 [2, 512], P('segment'), may hold values from 0.5 to 1.5
Outputs:
- section_out: bfloat16 [2, 32, 128, 512], P('segment', ('groups', 'lat'), 'lon'), parts along dimension 1
- boundary_grad: bfloat16 [2, 32, 128, 512], P('segment', ('groups', 'lat'), 'lon'), parts along dimension 1
- up_grad: float32 [4, 512, 2048], P(('groups', 'segment'), None, ('lon', 'lat')), parts along dimension 0
- down_grad: float32 [4, 2048, 512], P(('groups', 'segment'), ('lon', 'lat')), parts along dimension 0
- hidden_bias_grad: float32 [4, 2048], P(('groups', 'segment'), ('lon', 'lat')), parts along dimension 0
- kernel_grad: float32 [4, 49, 512], P(('groups', 'segment'), None, ('lon', 'lat')), parts along dimension 0
- vector_grad: float32 [4, 5, 512], P(('groups', 'segment'), None, ('lon', 'lat')), parts along dimension 0
The draws below stay inside these ranges and needn't reach their ends.
There are 2 independent parts, one for each index of `groups`. The reference program is written for one: setup_inputs(seed, part) draws one part's arguments, and reference() takes and returns one part's arrays. A program takes and returns all parts, laid end to end along the dimension named above; an argument that names none is the same for every part. Nothing has to cross between parts.
All inputs are finite; a program needn't handle non-finite values.
Results may differ from the reference program's by a relative error of at most 0.023.
Values may be sent and summed in bfloat16 or wider, within the bound.
A program may use at most 128 MiB of HBM per device.

```python
import math
import jax
import jax.numpy as jnp
from jax import lax

C = 512
HID = 2048
KERNEL = 7
SECTIONS = 2
LAT = 16
LON = 128


def spiked(values, own_key, source, target, shards_of, factor):
    def block_of(axis_at):
        return (jnp.arange(values.shape[axis_at]) // (values.shape[axis_at] // shards_of)).reshape((-1,) + (1,) * (values.ndim - 1 - axis_at))

    near = jax.random.permutation(own_key, shards_of)[block_of(target)]
    other_side = (block_of(target) + shards_of // 2) % shards_of
    return jnp.where((block_of(source) == near) | (block_of(source) == other_side), factor * values, values)


def block_scale(own_key, shape, pieces, smallest, high):
    level, own = 1.0, jax.random.fold_in(own_key, 6)
    for axis_at, shards_of in pieces:
        heights = jnp.exp(jax.random.uniform(jax.random.fold_in(own, axis_at), (shards_of,), jnp.float32, smallest / len(pieces), high / len(pieces)))
        level = level * jnp.repeat(heights, shape[axis_at] // shards_of).reshape([-1 if axis == axis_at else 1 for axis in range(len(shape))])
    return level


def scatter_about(stream_key, extent, width, limit, split=(), dtype=jnp.bfloat16):
    gain = block_scale(stream_key, extent, split, -0.22, 0.18) if split else 1.0
    array = jax.random.normal(stream_key, extent, jnp.float32) * width * gain
    return jnp.minimum(jnp.maximum(array, -limit), limit).astype(dtype)


def noise_with(rng, extent, deviation, reach, cuts, heavy, held_as=jnp.bfloat16):
    values = deviation * jax.random.normal(rng, extent, jnp.float32)
    if cuts:
        values = values * block_scale(rng, extent, cuts, -0.22, 0.18)
    return jnp.clip(spiked(values, jax.random.fold_in(rng, 3), *heavy), -reach, reach).astype(held_as)


def setup_inputs(seed: int = 0, part: int = 0) -> dict:
    key_list = jax.random.split(jax.random.key(seed), 12)
    part_keys = jax.random.split(jax.random.fold_in(key_list[11], part), 12)
    inputs = scatter_about(part_keys[0], (LAT, LON, C), 1.0, 6.0, ((0, 2), (1, 4)))
    cotangent = noise_with(part_keys[1], (LAT, LON, C), 1.0, 8.0, ((0, 2), (1, 4)), (1, 2, 4, 2.0))
    kernel = scatter_about(key_list[2], (SECTIONS, KERNEL * KERNEL, C), (KERNEL * KERNEL) ** -0.5, 0.875, ((0, 2),))
    conv_bias = scatter_about(key_list[3], (SECTIONS, C), 0.5, 3.0, ((0, 2),), jnp.float32)
    norm_gain = jnp.clip(jnp.exp(math.log(2.0) - 1.3862944 * jax.random.uniform(key_list[4], (SECTIONS, C), jnp.float32) ** block_scale(key_list[4], (SECTIONS, C), ((0, 2),), -0.2, 0.2)), 0.5, 2.0)
    norm_shift = scatter_about(key_list[5], (SECTIONS, C), 0.5, 3.0, ((0, 2),), jnp.float32)
    up_weight = scatter_about(key_list[6], (SECTIONS, C, HID), C ** -0.5, 0.25, ((0, 2),))
    hidden_bias = scatter_about(key_list[7], (SECTIONS, HID), 0.5, 3.0, ((0, 2),), jnp.float32)
    down_weight = scatter_about(key_list[8], (SECTIONS, HID, C), HID ** -0.5, 0.125, ((0, 2),))
    out_bias = scatter_about(key_list[9], (SECTIONS, C), 0.5, 3.0, ((0, 2),), jnp.float32)
    layer_scale = jnp.clip(0.5 + 1.0 * jax.random.uniform(key_list[10], (SECTIONS, C), jnp.float32) ** block_scale(key_list[10], (SECTIONS, C), ((0, 2),), -0.2, 0.2), 0.5, 1.5)
    return dict(inputs=inputs, cotangent=cotangent, kernel=kernel, conv_bias=conv_bias, norm_gain=norm_gain, norm_shift=norm_shift, up_weight=up_weight, hidden_bias=hidden_bias, down_weight=down_weight, out_bias=out_bias, layer_scale=layer_scale)


EPSILON = 1e-06
ROOT_HALF = 0.7071067811865476
DENSITY_SCALE = 0.3989422804014327

def extend_field(values):
    margin = KERNEL // 2
    half_turn = values.shape[1] // 2
    northern = jnp.roll(values[:margin][::-1], half_turn, axis=1)
    southern = jnp.roll(values[-margin:][::-1], half_turn, axis=1)
    lat_extended = jnp.concatenate([northern, values, southern], axis=0)
    return jnp.concatenate([lat_extended[:, -margin:], lat_extended, lat_extended[:, :margin]], axis=1)

def correlate(padded, stencil, out_rows, out_cols):
    accumulated = jnp.zeros((out_rows, out_cols, padded.shape[2]), jnp.float32)
    for row_tap in range(KERNEL):
        for col_tap in range(KERNEL):
            window = padded[row_tap:row_tap + out_rows, col_tap:col_tap + out_cols].astype(jnp.float32)
            accumulated = accumulated + window * stencil[row_tap, col_tap].astype(jnp.float32)
    return accumulated

def stencil_terms(padded, grad_low, out_rows, out_cols):
    grad_wide = grad_low.astype(jnp.float32)
    columns = []
    for row_tap in range(KERNEL):
        for col_tap in range(KERNEL):
            window = padded[row_tap:row_tap + out_rows, col_tap:col_tap + out_cols].astype(jnp.float32)
            columns.append(lax.optimization_barrier(jnp.sum(window * grad_wide, axis=(0, 1))))
    return jnp.stack(columns)

def gelu_parts(before):
    cumulative = 0.5 * (1.0 + lax.erf(before * ROOT_HALF))
    density = jnp.exp(-0.5 * before * before) * DENSITY_SCALE
    return (before * cumulative, cumulative + before * density)

def forward_section(values, padded, params):
    stencil, conv_bias, norm_gain, norm_shift, up_matrix, bias_hidden, down_matrix, bias_out, scaling = params
    out_rows, out_cols, channels = values.shape
    stencil_grid = stencil.reshape(KERNEL, KERNEL, channels)
    activity = correlate(padded, stencil_grid, out_rows, out_cols) + conv_bias
    average = lax.optimization_barrier(jnp.mean(activity, axis=-1, keepdims=True))
    centred = activity - average
    variance = lax.optimization_barrier(jnp.mean(centred * centred, axis=-1, keepdims=True))
    inverse = lax.rsqrt(variance + EPSILON)
    unit_norm = centred * inverse
    normed = (unit_norm * norm_gain + norm_shift).astype(jnp.bfloat16).reshape(out_rows * out_cols, channels)
    before = jnp.dot(normed, up_matrix, preferred_element_type=jnp.float32) + bias_hidden
    activated, slope_value = gelu_parts(before)
    hidden = activated.astype(jnp.bfloat16)
    branch = jnp.dot(hidden, down_matrix, preferred_element_type=jnp.float32) + bias_out
    result = (values.astype(jnp.float32) + scaling * branch.reshape(out_rows, out_cols, channels)).astype(jnp.bfloat16)
    return (result, (padded, unit_norm, inverse, normed, slope_value, hidden, branch))

def backward_section(stored, upstream, params, extender, north_weight, south_weight):
    padded, unit_norm, inverse, normed, slope_value, hidden, branch = stored
    stencil, conv_bias, norm_gain, norm_shift, up_matrix, bias_hidden, down_matrix, bias_out, scaling = params
    out_rows, out_cols, channels = upstream.shape
    margin = KERNEL // 2
    incoming = upstream.astype(jnp.float32)
    incoming_flat = incoming.reshape(out_rows * out_cols, channels)
    scale_grad = lax.optimization_barrier(jnp.sum(incoming_flat * branch, axis=0))
    scaled = (incoming_flat * scaling).astype(jnp.bfloat16)
    bias_out_grad = lax.optimization_barrier(jnp.sum(scaled.astype(jnp.float32), axis=0))
    down_sum = jnp.dot(hidden.T, scaled, preferred_element_type=jnp.float32)
    hidden_grad = jnp.dot(scaled, down_matrix.T, preferred_element_type=jnp.float32)
    before_grad = (hidden_grad * slope_value).astype(jnp.bfloat16)
    up_sum = jnp.dot(normed.T, before_grad, preferred_element_type=jnp.float32)
    bias_sum = lax.optimization_barrier(jnp.sum(before_grad.astype(jnp.float32), axis=0))
    normed_grad = jnp.dot(before_grad, up_matrix.T, preferred_element_type=jnp.float32).reshape(out_rows, out_cols, channels)
    gain_grad = lax.optimization_barrier(jnp.sum(normed_grad * unit_norm, axis=(0, 1)))
    shift_grad = lax.optimization_barrier(jnp.sum(normed_grad, axis=(0, 1)))
    gained = normed_grad * norm_gain
    activity_grad = inverse * (gained - lax.optimization_barrier(jnp.mean(gained, axis=-1, keepdims=True)) - unit_norm * lax.optimization_barrier(jnp.mean(gained * unit_norm, axis=-1, keepdims=True)))
    activity_low = activity_grad.astype(jnp.bfloat16)
    conv_bias_grad = lax.optimization_barrier(jnp.sum(activity_low.astype(jnp.float32), axis=(0, 1)))
    stencil_sum = stencil_terms(padded, activity_low, out_rows, out_cols)
    spread = extender(activity_low)
    stencil_grid = stencil.reshape(KERNEL, KERNEL, channels).astype(jnp.float32)
    flipped = stencil_grid[::-1, ::-1]
    correction = stencil_grid[:, ::-1] - flipped
    through = correlate(spread, flipped, out_rows, out_cols)
    zero_rows = jnp.zeros_like(spread[:2 * margin])
    top_part = jnp.concatenate([spread[:margin], zero_rows], axis=0)
    bottom_part = jnp.concatenate([zero_rows, spread[-margin:]], axis=0)
    top_fix = correlate(top_part, correction, margin, out_cols) * north_weight
    bottom_fix = correlate(bottom_part, correction, margin, out_cols) * south_weight
    rest_rows = out_rows - margin
    top_full = jnp.pad(top_fix, ((0, rest_rows), (0, 0), (0, 0)))
    bottom_full = jnp.pad(bottom_fix, ((rest_rows, 0), (0, 0), (0, 0)))
    through = through + top_full + bottom_full
    passed = (incoming + through).astype(jnp.bfloat16)
    vectors = jnp.stack([conv_bias_grad, gain_grad, shift_grad, bias_out_grad, scale_grad])
    return (passed, (up_sum, down_sum, bias_sum, stencil_sum, vectors))

def reference(inputs, cotangent, kernel, conv_bias, norm_gain, norm_shift, up_weight, hidden_bias, down_weight, out_bias, layer_scale):

    def section_params(index):
        return (kernel[index], conv_bias[index], norm_gain[index], norm_shift[index], up_weight[index], hidden_bias[index], down_weight[index], out_bias[index], layer_scale[index])
    first_out, first_stored = forward_section(inputs, extend_field(inputs), section_params(0))
    second_out, second_stored = forward_section(first_out, extend_field(first_out), section_params(1))
    second_grad, second_sums = backward_section(second_stored, cotangent, section_params(1), extend_field, 1.0, 1.0)
    first_grad, first_sums = backward_section(first_stored, second_grad, section_params(0), extend_field, 1.0, 1.0)
    return (jnp.stack([first_out, second_out]), jnp.stack([first_grad, second_grad]), jnp.stack([first_sums[0], second_sums[0]]), jnp.stack([first_sums[1], second_sums[1]]), jnp.stack([first_sums[2], second_sums[2]]), jnp.stack([first_sums[3], second_sums[3]]), jnp.stack([first_sums[4], second_sums[4]]))
```

```python
import jax
import jax.numpy as jnp
from jax import lax
from jax.sharding import PartitionSpec as P

KERNEL = 7


EPSILON = 1e-06
ROOT_HALF = 0.7071067811865476
DENSITY_SCALE = 0.3989422804014327


def extended(cells, sides, width, closed):
    for axis, dim in sides:
        count = lax.axis_size(axis)
        ends = count if closed else count - 1
        head = lax.slice_in_dim(cells, 0, width, axis=dim)
        tail = lax.slice_in_dim(cells, cells.shape[dim] - width, cells.shape[dim], axis=dim)
        cells = jnp.concatenate(
            [
                lax.ppermute(tail, axis, [(i, (i + 1) % count) for i in range(ends)]),
                cells,
                lax.ppermute(head, axis, [((i + 1) % count, i) for i in range(ends)]),
            ],
            axis=dim,
        )
    return cells


def from_behind(value, axis, steps):
    count = lax.axis_size(axis)
    pairs = [(source, (source + steps) % count) for source in range(count)]
    return lax.ppermute(value, axis, pairs)


def partner_2(shard, axis, apart):
    return lax.ppermute(shard, axis, [(i, i ^ 1 << apart) for i in range(lax.axis_size(axis))])


def correlate(padded, stencil, out_rows, out_cols):
    accumulated = jnp.zeros((out_rows, out_cols, padded.shape[2]), jnp.float32)
    for row_tap in range(KERNEL):
        for col_tap in range(KERNEL):
            window = padded[row_tap : row_tap + out_rows, col_tap : col_tap + out_cols].astype(
                jnp.float32
            )
            accumulated = accumulated + window * stencil[row_tap, col_tap].astype(jnp.float32)
    return accumulated


def stencil_terms(padded, grad_low, out_rows, out_cols):
    grad_wide = grad_low.astype(jnp.float32)
    columns = []
    for row_tap in range(KERNEL):
        for col_tap in range(KERNEL):
            window = padded[row_tap : row_tap + out_rows, col_tap : col_tap + out_cols].astype(
                jnp.float32
            )
            columns.append(jnp.sum(window * grad_wide, axis=(0, 1)))
    return jnp.stack(columns)


def gelu_parts(before):
    cumulative = 0.5 * (1.0 + lax.erf(before * ROOT_HALF))
    density = jnp.exp(-0.5 * before * before) * DENSITY_SCALE
    return (before * cumulative, cumulative + before * density)


def forward_section(values, padded, params):
    (
        stencil,
        conv_bias,
        norm_gain,
        norm_shift,
        up_matrix,
        bias_hidden,
        down_matrix,
        bias_out,
        scaling,
    ) = params
    out_rows, out_cols, channels = values.shape
    stencil_grid = stencil.reshape(KERNEL, KERNEL, channels)
    activity = correlate(padded, stencil_grid, out_rows, out_cols) + conv_bias
    average = jnp.mean(activity, axis=-1, keepdims=True)
    centred = activity - average
    variance = jnp.mean(centred * centred, axis=-1, keepdims=True)
    inverse = lax.rsqrt(variance + EPSILON)
    unit_norm = centred * inverse
    normed = (
        (unit_norm * norm_gain + norm_shift)
        .astype(jnp.bfloat16)
        .reshape(out_rows * out_cols, channels)
    )
    before = jnp.dot(normed, up_matrix, preferred_element_type=jnp.float32) + bias_hidden
    activated, slope_value = gelu_parts(before)
    hidden = activated.astype(jnp.bfloat16)
    branch = jnp.dot(hidden, down_matrix, preferred_element_type=jnp.float32) + bias_out
    result = (
        values.astype(jnp.float32) + scaling * branch.reshape(out_rows, out_cols, channels)
    ).astype(jnp.bfloat16)
    return (result, (padded, unit_norm, inverse, normed, slope_value, hidden, branch))


def backward_section(stored, upstream, params, extender, north_weight, south_weight):
    padded, unit_norm, inverse, normed, slope_value, hidden, branch = stored
    (
        stencil,
        conv_bias,
        norm_gain,
        norm_shift,
        up_matrix,
        bias_hidden,
        down_matrix,
        bias_out,
        scaling,
    ) = params
    out_rows, out_cols, channels = upstream.shape
    margin = KERNEL // 2
    incoming = upstream.astype(jnp.float32)
    incoming_flat = incoming.reshape(out_rows * out_cols, channels)
    scale_grad = jnp.sum(incoming_flat * branch, axis=0)
    scaled = (incoming_flat * scaling).astype(jnp.bfloat16)
    bias_out_grad = jnp.sum(scaled.astype(jnp.float32), axis=0)
    down_sum = jnp.dot(hidden.T, scaled, preferred_element_type=jnp.float32)
    hidden_grad = jnp.dot(scaled, down_matrix.T, preferred_element_type=jnp.float32)
    before_grad = (hidden_grad * slope_value).astype(jnp.bfloat16)
    up_sum = jnp.dot(normed.T, before_grad, preferred_element_type=jnp.float32)
    bias_sum = jnp.sum(before_grad.astype(jnp.float32), axis=0)
    normed_grad = jnp.dot(before_grad, up_matrix.T, preferred_element_type=jnp.float32).reshape(
        out_rows, out_cols, channels
    )
    gain_grad = jnp.sum(normed_grad * unit_norm, axis=(0, 1))
    shift_grad = jnp.sum(normed_grad, axis=(0, 1))
    gained = normed_grad * norm_gain
    activity_grad = inverse * (
        gained
        - jnp.mean(gained, axis=-1, keepdims=True)
        - unit_norm * jnp.mean(gained * unit_norm, axis=-1, keepdims=True)
    )
    activity_low = activity_grad.astype(jnp.bfloat16)
    conv_bias_grad = jnp.sum(activity_low.astype(jnp.float32), axis=(0, 1))
    stencil_sum = stencil_terms(padded, activity_low, out_rows, out_cols)
    spread = extender(activity_low)
    stencil_grid = stencil.reshape(KERNEL, KERNEL, channels).astype(jnp.float32)
    flipped = stencil_grid[::-1, ::-1]
    correction = stencil_grid[:, ::-1] - flipped
    through = correlate(spread, flipped, out_rows, out_cols)
    zero_rows = jnp.zeros_like(spread[: 2 * margin])
    top_part = jnp.concatenate([spread[:margin], zero_rows], axis=0)
    bottom_part = jnp.concatenate([zero_rows, spread[-margin:]], axis=0)
    top_fix = correlate(top_part, correction, margin, out_cols) * north_weight
    bottom_fix = correlate(bottom_part, correction, margin, out_cols) * south_weight
    rest_rows = out_rows - margin
    top_full = jnp.pad(top_fix, ((0, rest_rows), (0, 0), (0, 0)))
    bottom_full = jnp.pad(bottom_fix, ((rest_rows, 0), (0, 0), (0, 0)))
    through = through + top_full + bottom_full
    passed = (incoming + through).astype(jnp.bfloat16)
    vectors = jnp.stack([conv_bias_grad, gain_grad, shift_grad, bias_out_grad, scale_grad])
    return (passed, (up_sum, down_sum, bias_sum, stencil_sum, vectors))


def lat_neighbours(edge_rows):
    return extended(edge_rows, (("lat", 0),), KERNEL // 2, False)


CYCLE = ("lon", "segment")


def lon_neighbours(edge_cols):
    return extended(edge_cols, ((CYCLE, 1),), KERNEL // 2, True)


def pole_partner(edge_rows):
    return from_behind(edge_rows, CYCLE, lax.axis_size(CYCLE) // 2)


def hand_over(values):
    return partner_2(values, "segment", 0)


def extend_local(values, northern, southern, row_source):
    margin = KERNEL // 2
    edge_rows = jnp.concatenate([values[:margin], values[-margin:]], axis=0)
    nearby = row_source(edge_rows)
    partner = pole_partner(edge_rows)
    upper_rows = jnp.where(northern, partner[:margin][::-1], nearby[:margin])
    lower_rows = jnp.where(southern, partner[margin:][::-1], nearby[-margin:])
    lat_extended = jnp.concatenate([upper_rows, values, lower_rows], axis=0)
    edge_cols = jnp.concatenate([lat_extended[:, :margin], lat_extended[:, -margin:]], axis=1)
    beside_all = lon_neighbours(edge_cols)
    return jnp.concatenate([beside_all[:, :margin], lat_extended, beside_all[:, -margin:]], axis=1)


def both_halves(leading, first, second, dim):
    received = hand_over(jnp.where(leading, second, first))
    own = jnp.where(leading, first, second)
    return jnp.where(
        leading,
        jnp.concatenate([own, received], axis=dim),
        jnp.concatenate([received, own], axis=dim),
    )


def scattered(value, dim):
    return lax.psum_scatter(
        value.astype(jnp.bfloat16), ("lon", "lat", "segment"), scatter_dimension=dim, tiled=True
    )


def packed(sums):
    _, _, bias_sum, stencil_sum, vectors = sums
    channels = vectors.shape[1]
    pieces = lax.axis_size(("lon", "lat"))
    bias_rows = (
        bias_sum.reshape(pieces, -1, channels // pieces).transpose(1, 0, 2).reshape(-1, channels)
    )
    return jnp.concatenate([stencil_sum, vectors, bias_rows], axis=0)


def local(
    inputs,
    cotangent,
    kernel,
    conv_bias,
    norm_gain,
    norm_shift,
    up_weight,
    hidden_bias,
    down_weight,
    out_bias,
    layer_scale,
):
    core = lax.axis_index("segment")
    leading = core == 0
    width = inputs.shape[1] // lax.axis_size("segment")
    channels = inputs.shape[2]
    inputs = lax.dynamic_slice_in_dim(inputs, core * width, width, axis=1)
    cotangent = lax.dynamic_slice_in_dim(cotangent, core * width, width, axis=1)
    rows = jnp.concatenate(
        [conv_bias, norm_gain, norm_shift, out_bias, layer_scale, hidden_bias.reshape(-1, channels)],
        axis=0,
    )
    taps, rows, ups, downs = [
        lax.all_gather(value, "segment", axis=0)
        for value in (kernel[0], rows, up_weight[0], down_weight[0])
    ]
    sections = [
        (
            taps[s],
            rows[s, 0],
            rows[s, 1],
            rows[s, 2],
            ups[s],
            rows[s, 5:].reshape(-1),
            downs[s],
            rows[s, 3],
            rows[s, 4],
        )
        for s in range(2)
    ]
    northern = lax.axis_index("lat") == 0
    southern = lax.axis_index("lat") == lax.axis_size("lat") - 1
    north_weight = jnp.where(northern, 1.0, 0.0).astype(jnp.float32)
    south_weight = jnp.where(southern, 1.0, 0.0).astype(jnp.float32)

    def extender(values):
        return extend_local(values, northern, southern, lat_neighbours)

    first_out, first_stored = forward_section(inputs, extender(inputs), sections[0])
    second_out, second_stored = forward_section(first_out, extender(first_out), sections[1])
    second_grad, second_sums = backward_section(
        second_stored, cotangent, sections[1], extender, north_weight, south_weight
    )
    up_second = scattered(second_sums[0], 1)
    down_second = scattered(second_sums[1], 0)
    first_grad, first_sums = backward_section(
        first_stored, second_grad, sections[0], extender, north_weight, south_weight
    )
    up_first = scattered(first_sums[0], 1)
    down_first = scattered(first_sums[1], 0)
    section_out = both_halves(leading, first_out, second_out, 1)[None]
    boundary_grad = both_halves(leading, first_grad, second_grad, 1)[None]
    up_part = both_halves(leading, up_first, up_second, 1).astype(jnp.float32)
    down_part = both_halves(leading, down_first, down_second, 0).astype(jnp.float32)
    first_small = packed(first_sums)
    second_small = packed(second_sums)
    small = jnp.where(leading, first_small, second_small) + hand_over(
        jnp.where(leading, second_small, first_small)
    )
    small = lax.psum_scatter(
        small.astype(jnp.bfloat16), ("lon", "lat"), scatter_dimension=1, tiled=True
    ).astype(jnp.float32)
    count = KERNEL * KERNEL
    stencil_part = small[:count]
    vector_part = small[count : count + 5]
    bias_part = small[count + 5 :].reshape(-1)
    return (
        section_out,
        boundary_grad,
        up_part[None],
        down_part[None],
        bias_part[None],
        stencil_part[None],
        vector_part[None],
    )


def solution(mesh):
    placed = (
        P(("groups", "lat"), "lon", None),
        P(("groups", "lat"), "lon", None),
        P("segment", None, None),
        P("segment", None),
        P("segment", None),
        P("segment", None),
        P("segment", None, None),
        P("segment", None),
        P("segment", None, None),
        P("segment", None),
        P("segment", None),
    )
    return jax.shard_map(
        local,
        mesh=mesh,
        in_specs=placed,
        out_specs=(
            P("segment", ("groups", "lat"), "lon", None),
            P("segment", ("groups", "lat"), "lon", None),
            P(("groups", "segment"), None, ("lon", "lat")),
            P(("groups", "segment"), ("lon", "lat"), None),
            P(("groups", "segment"), ("lon", "lat")),
            P(("groups", "segment"), None, ("lon", "lat")),
            P(("groups", "segment"), None, ("lon", "lat")),
        ),
        check_vma=False,
    )
```

```python
import functools
import jax
import jax.numpy as jnp
from jax import lax
from jax.experimental import pallas as pl
from jax.experimental.pallas import tpu as pltpu
from jax.sharding import PartitionSpec as P

KERNEL = 7


EPSILON = 1e-06
ROOT_HALF = 0.7071067811865476
DENSITY_SCALE = 0.3989422804014327


def extended(cells, sides, width, closed):
    for axis, dim in sides:
        count = lax.axis_size(axis)
        ends = count if closed else count - 1
        head = lax.slice_in_dim(cells, 0, width, axis=dim)
        tail = lax.slice_in_dim(cells, cells.shape[dim] - width, cells.shape[dim], axis=dim)
        cells = jnp.concatenate(
            [
                lax.ppermute(tail, axis, [(i, (i + 1) % count) for i in range(ends)]),
                cells,
                lax.ppermute(head, axis, [((i + 1) % count, i) for i in range(ends)]),
            ],
            axis=dim,
        )
    return cells


def from_behind(value, axis, steps):
    count = lax.axis_size(axis)
    pairs = [(source, (source + steps) % count) for source in range(count)]
    return lax.ppermute(value, axis, pairs)


def partner_2(shard, axis, apart):
    return lax.ppermute(shard, axis, [(i, i ^ 1 << apart) for i in range(lax.axis_size(axis))])


def correlate(padded, stencil, out_rows, out_cols):
    accumulated = jnp.zeros((out_rows, out_cols, padded.shape[2]), jnp.float32)
    for row_tap in range(KERNEL):
        for col_tap in range(KERNEL):
            window = padded[row_tap : row_tap + out_rows, col_tap : col_tap + out_cols].astype(
                jnp.float32
            )
            accumulated = accumulated + window * stencil[row_tap, col_tap].astype(jnp.float32)
    return accumulated


def stencil_terms(padded, grad_low, out_rows, out_cols):
    grad_wide = grad_low.astype(jnp.float32)
    columns = []
    for row_tap in range(KERNEL):
        for col_tap in range(KERNEL):
            window = padded[row_tap : row_tap + out_rows, col_tap : col_tap + out_cols].astype(
                jnp.float32
            )
            columns.append(jnp.sum(window * grad_wide, axis=(0, 1)))
    return jnp.stack(columns)


def gelu_parts(before):
    cumulative = 0.5 * (1.0 + lax.erf(before * ROOT_HALF))
    density = jnp.exp(-0.5 * before * before) * DENSITY_SCALE
    return (before * cumulative, cumulative + before * density)


def forward_section(values, padded, params):
    (
        stencil,
        conv_bias,
        norm_gain,
        norm_shift,
        up_matrix,
        bias_hidden,
        down_matrix,
        bias_out,
        scaling,
    ) = params
    out_rows, out_cols, channels = values.shape
    stencil_grid = stencil.reshape(KERNEL, KERNEL, channels)
    activity = correlate(padded, stencil_grid, out_rows, out_cols) + conv_bias
    average = jnp.mean(activity, axis=-1, keepdims=True)
    centred = activity - average
    variance = jnp.mean(centred * centred, axis=-1, keepdims=True)
    inverse = lax.rsqrt(variance + EPSILON)
    unit_norm = centred * inverse
    normed = (
        (unit_norm * norm_gain + norm_shift)
        .astype(jnp.bfloat16)
        .reshape(out_rows * out_cols, channels)
    )
    before = jnp.dot(normed, up_matrix, preferred_element_type=jnp.float32) + bias_hidden
    activated, slope_value = gelu_parts(before)
    hidden = activated.astype(jnp.bfloat16)
    branch = jnp.dot(hidden, down_matrix, preferred_element_type=jnp.float32) + bias_out
    result = (
        values.astype(jnp.float32) + scaling * branch.reshape(out_rows, out_cols, channels)
    ).astype(jnp.bfloat16)
    return (result, (padded, unit_norm, inverse, normed, slope_value, hidden, branch))


def backward_section(stored, upstream, params, extender, north_weight, south_weight):
    padded, unit_norm, inverse, normed, slope_value, hidden, branch = stored
    (
        stencil,
        conv_bias,
        norm_gain,
        norm_shift,
        up_matrix,
        bias_hidden,
        down_matrix,
        bias_out,
        scaling,
    ) = params
    out_rows, out_cols, channels = upstream.shape
    margin = KERNEL // 2
    incoming = upstream.astype(jnp.float32)
    incoming_flat = incoming.reshape(out_rows * out_cols, channels)
    scale_grad = jnp.sum(incoming_flat * branch, axis=0)
    scaled = (incoming_flat * scaling).astype(jnp.bfloat16)
    bias_out_grad = jnp.sum(scaled.astype(jnp.float32), axis=0)
    down_sum = jnp.dot(hidden.T, scaled, preferred_element_type=jnp.float32)
    hidden_grad = jnp.dot(scaled, down_matrix.T, preferred_element_type=jnp.float32)
    before_grad = (hidden_grad * slope_value).astype(jnp.bfloat16)
    up_sum = jnp.dot(before_grad.T, normed, preferred_element_type=jnp.float32)
    bias_sum = jnp.sum(before_grad.astype(jnp.float32), axis=0)
    normed_grad = jnp.dot(before_grad, up_matrix.T, preferred_element_type=jnp.float32).reshape(
        out_rows, out_cols, channels
    )
    gain_grad = jnp.sum(normed_grad * unit_norm, axis=(0, 1))
    shift_grad = jnp.sum(normed_grad, axis=(0, 1))
    gained = normed_grad * norm_gain
    activity_grad = inverse * (
        gained
        - jnp.mean(gained, axis=-1, keepdims=True)
        - unit_norm * jnp.mean(gained * unit_norm, axis=-1, keepdims=True)
    )
    activity_low = activity_grad.astype(jnp.bfloat16)
    conv_bias_grad = jnp.sum(activity_low.astype(jnp.float32), axis=(0, 1))
    stencil_sum = stencil_terms(padded, activity_low, out_rows, out_cols)
    spread = extender(activity_low)
    stencil_grid = stencil.reshape(KERNEL, KERNEL, channels).astype(jnp.float32)
    flipped = stencil_grid[::-1, ::-1]
    correction = stencil_grid[:, ::-1] - flipped
    through = correlate(spread, flipped, out_rows, out_cols)
    zero_rows = jnp.zeros_like(spread[: 2 * margin])
    top_part = jnp.concatenate([spread[:margin], zero_rows], axis=0)
    bottom_part = jnp.concatenate([zero_rows, spread[-margin:]], axis=0)
    top_fix = correlate(top_part, correction, margin, out_cols) * north_weight
    bottom_fix = correlate(bottom_part, correction, margin, out_cols) * south_weight
    rest_rows = out_rows - margin
    top_full = jnp.pad(top_fix, ((0, rest_rows), (0, 0), (0, 0)))
    bottom_full = jnp.pad(bottom_fix, ((rest_rows, 0), (0, 0), (0, 0)))
    through = through + top_full + bottom_full
    passed = (incoming + through).astype(jnp.bfloat16)
    vectors = jnp.stack([conv_bias_grad, gain_grad, shift_grad, bias_out_grad, scale_grad])
    return (passed, (up_sum, down_sum, bias_sum, stencil_sum, vectors))


def lat_neighbours(edge_rows):
    return extended(edge_rows, (("lat", 0),), KERNEL // 2, False)


CYCLE = ("lon", "segment")


def lon_neighbours(edge_cols):
    return extended(edge_cols, ((CYCLE, 1),), KERNEL // 2, True)


def pole_partner(edge_rows):
    return from_behind(edge_rows, CYCLE, lax.axis_size(CYCLE) // 2)


def hand_over(values):
    return partner_2(values, "segment", 0)


def extend_local(values, northern, southern, row_source):
    margin = KERNEL // 2
    edge_rows = jnp.concatenate([values[:margin], values[-margin:]], axis=0)
    nearby = row_source(edge_rows)
    partner = pole_partner(edge_rows)
    upper_rows = jnp.where(northern, partner[:margin][::-1], nearby[:margin])
    lower_rows = jnp.where(southern, partner[margin:][::-1], nearby[-margin:])
    lat_extended = jnp.concatenate([upper_rows, values, lower_rows], axis=0)
    edge_cols = jnp.concatenate([lat_extended[:, :margin], lat_extended[:, -margin:]], axis=1)
    beside_all = lon_neighbours(edge_cols)
    return jnp.concatenate([beside_all[:, :margin], lat_extended, beside_all[:, -margin:]], axis=1)


def both_halves(leading, first, second, dim):
    received = hand_over(jnp.where(leading, second, first))
    own = jnp.where(leading, first, second)
    return jnp.where(
        leading,
        jnp.concatenate([own, received], axis=dim),
        jnp.concatenate([received, own], axis=dim),
    )


def plan(lon, lat):
    lon_bits, lat_bits = lon.bit_length() - 1, lat.bit_length() - 1
    along_lon = [("lon", bit, lon_bits - 1 - bit) for bit in range(lon_bits)]
    along_lat = [("lat", bit, lon_bits + lat_bits - 1 - bit) for bit in range(lat_bits)]
    first = along_lat + along_lon
    second = along_lon[:1] + along_lat + along_lon[1:]
    return first, second


def picked(axis, bit):
    return (slice(None),) * axis + (bit,)


def add_block(total, term, lead):
    rows = total.shape[-2]
    step = min(rows, 64)
    per = rows // step
    count = per
    for size in lead:
        count = count * size

    def body(at, carry):
        row = pl.multiple_of((at % per) * step, step)
        rest = at // per
        index = []
        for size in reversed(lead):
            index.insert(0, rest % size)
            rest = rest // size
        term(tuple(index), pl.ds(row, step))
        return carry

    lax.fori_loop(0, count, body, 0)


def reduce_kernel(orders, depth, *refs):
    parts = len(orders)
    first, second = refs[:parts], refs[parts : 2 * parts]
    outs = refs[2 * parts : 3 * parts]
    slots = [refs[3 * parts + p * (depth + 1) : 3 * parts + (p + 1) * (depth + 1)] for p in range(parts)]
    send_sem, recv_sem = refs[3 * parts + parts * (depth + 1) :]
    core = lax.axis_index("segment")
    place = {"lon": lax.axis_index("lon"), "lat": lax.axis_index("lat")}

    def bit_of(step):
        return (place[step[0]] // (1 << step[1])) % 2

    def across(step):
        own = bit_of(step)
        return {step[0]: place[step[0]] + (1 - 2 * own) * (1 << step[1])}

    barrier = pltpu.get_barrier_semaphore()
    pl.semaphore_signal(
        barrier, inc=1, device_id={"segment": 1 - core}, device_id_type=pl.DeviceIdType.MESH
    )
    for step in orders[0]:
        pl.semaphore_signal(
            barrier, inc=1, device_id=across(step), device_id_type=pl.DeviceIdType.MESH
        )
    pl.semaphore_wait(barrier, depth + 1)

    def chip_copy(part, half, source):
        step = orders[part][0]
        bit = bit_of(step)
        index = picked(step[2], 1 - bit if half == 0 else bit)
        return pltpu.make_async_remote_copy(
            src_ref=source.at[index],
            dst_ref=slots[part][0].at[index],
            send_sem=send_sem.at[part, half],
            recv_sem=recv_sem.at[part, half],
            device_id={"segment": 1 - core},
            device_id_type=pl.DeviceIdType.MESH,
        )

    def axis_copy(part, stage):
        step = orders[part][stage]
        position = step[2] - sum(1 for done in orders[part][:stage] if done[2] < step[2])
        return pltpu.make_async_remote_copy(
            src_ref=slots[part][stage].at[picked(position, 1 - bit_of(step))],
            dst_ref=slots[part][stage + 1],
            send_sem=send_sem.at[part, 2 + stage],
            recv_sem=recv_sem.at[part, 2 + stage],
            device_id=across(step),
            device_id_type=pl.DeviceIdType.MESH,
        )

    def position_of(part, stage):
        step = orders[part][stage]
        return step[2] - sum(1 for done in orders[part][:stage] if done[2] < step[2])

    def add_into(target, source, fixed_at, bit, source_at, source_bit):
        lead = target.shape[:-2]
        if fixed_at is not None:
            lead = lead[:fixed_at] + lead[fixed_at + 1 :]

        def term(index, rows):
            full = index
            if fixed_at is not None:
                full = index[:fixed_at] + (bit,) + index[fixed_at:]
            taken = full
            if source_at is not None:
                taken = full[:source_at] + (source_bit,) + full[source_at:]
            spot = full + (rows, slice(None))
            total = target[spot].astype(jnp.float32) + source[
                taken + (rows, slice(None))
            ].astype(jnp.float32)
            target[spot] = total.astype(target.dtype)

        add_block(target, term, lead)

    for half in range(2):
        for part in range(parts):

            @pl.when(core == 0)
            def _():
                chip_copy(part, half, second[part]).start()

            @pl.when(core == 1)
            def _():
                chip_copy(part, half, first[part]).start()

    for half in range(2):
        for part in range(parts):
            step = orders[part][0]
            bit = bit_of(step)
            bit = 1 - bit if half == 0 else bit
            chip_copy(part, half, first[part]).wait_recv()

            @pl.when(core == 0)
            def _():
                add_into(slots[part][0], first[part], step[2], bit, None, None)

            @pl.when(core == 1)
            def _():
                add_into(slots[part][0], second[part], step[2], bit, None, None)

            if half == 0:
                axis_copy(part, 0).start()

    for stage in range(depth):
        for part in range(parts):
            step = orders[part][stage]
            source_at, own = position_of(part, stage), bit_of(step)
            axis_copy(part, stage).wait_recv()
            source, target = slots[part][stage], slots[part][stage + 1]
            if stage + 1 < depth:
                fixed_at, bit = position_of(part, stage + 1), bit_of(orders[part][stage + 1])
                add_into(target, source, fixed_at, 1 - bit, source_at, own)
                axis_copy(part, stage + 1).start()
                add_into(target, source, fixed_at, bit, source_at, own)
            else:
                outs[part][...] = target[...].astype(jnp.float32) + source[
                    picked(source_at, own)
                ].astype(jnp.float32)
    for part in range(parts):
        for half in range(2):
            chip_copy(part, half, first[part]).wait_send()
        for stage in range(depth):
            axis_copy(part, stage).wait_send()


def reduced(first, second):
    lon, lat = lax.axis_size("lon"), lax.axis_size("lat")
    order_a, order_b = plan(lon, lat)
    orders = (order_a, order_b, order_a)
    depth = len(order_a)
    lead = (2,) * depth
    first = [value.astype(jnp.bfloat16).reshape(lead + value.shape[1:]) for value in first]
    second = [value.astype(jnp.bfloat16).reshape(lead + value.shape[1:]) for value in second]
    blocks = [value.shape[depth:] for value in first]
    scratch = [
        pltpu.VMEM((2,) * (depth - stage) + block, jnp.bfloat16)
        for block in blocks
        for stage in range(depth + 1)
    ]
    vmem = pl.BlockSpec(memory_space=pltpu.VMEM)
    return pl.pallas_call(
        functools.partial(reduce_kernel, orders, depth),
        out_shape=[jax.ShapeDtypeStruct(block, jnp.float32) for block in blocks],
        in_specs=[vmem] * (2 * len(blocks)),
        out_specs=[vmem] * len(blocks),
        scratch_shapes=scratch
        + [
            pltpu.SemaphoreType.DMA((len(blocks), depth + 2)),
            pltpu.SemaphoreType.DMA((len(blocks), depth + 2)),
        ],
        compiler_params=pltpu.CompilerParams(
            collective_id=0, has_side_effects=True, vmem_limit_bytes=48 * 1024 * 1024
        ),
    )(*first, *second)


def packed(sums):
    _, _, bias_sum, stencil_sum, vectors = sums
    channels = vectors.shape[1]
    pieces = lax.axis_size(("lon", "lat"))
    bias_rows = (
        bias_sum.reshape(pieces, -1, channels // pieces).transpose(1, 0, 2).reshape(-1, channels)
    )
    rows = jnp.concatenate([stencil_sum, vectors, bias_rows], axis=0)
    rows = rows.reshape(rows.shape[0], pieces, channels // pieces).transpose(1, 0, 2)
    return jnp.pad(rows, ((0, 0), (0, -rows.shape[1] % 16), (0, -rows.shape[2] % 128)))


def chunked(sums):
    pieces = lax.axis_size(("lon", "lat"))
    up_sum, down_sum = sums[:2]
    return (
        up_sum.reshape(pieces, -1, up_sum.shape[1]),
        down_sum.reshape(pieces, -1, down_sum.shape[1]),
        packed(sums),
    )


def local(
    inputs,
    cotangent,
    kernel,
    conv_bias,
    norm_gain,
    norm_shift,
    up_weight,
    hidden_bias,
    down_weight,
    out_bias,
    layer_scale,
):
    core = lax.axis_index("segment")
    leading = core == 0
    width = inputs.shape[1] // lax.axis_size("segment")
    channels = inputs.shape[2]
    inputs = lax.dynamic_slice_in_dim(inputs, core * width, width, axis=1)
    cotangent = lax.dynamic_slice_in_dim(cotangent, core * width, width, axis=1)
    rows = jnp.concatenate(
        [conv_bias, norm_gain, norm_shift, out_bias, layer_scale, hidden_bias.reshape(-1, channels)],
        axis=0,
    )
    taps, rows, ups, downs = [
        lax.all_gather(value, "segment", axis=0)
        for value in (kernel[0], rows, up_weight[0], down_weight[0])
    ]
    sections = [
        (
            taps[s],
            rows[s, 0],
            rows[s, 1],
            rows[s, 2],
            ups[s],
            rows[s, 5:].reshape(-1),
            downs[s],
            rows[s, 3],
            rows[s, 4],
        )
        for s in range(2)
    ]
    northern = lax.axis_index("lat") == 0
    southern = lax.axis_index("lat") == lax.axis_size("lat") - 1
    north_weight = jnp.where(northern, 1.0, 0.0).astype(jnp.float32)
    south_weight = jnp.where(southern, 1.0, 0.0).astype(jnp.float32)

    def extender(values):
        return extend_local(values, northern, southern, lat_neighbours)

    first_out, first_stored = forward_section(inputs, extender(inputs), sections[0])
    second_out, second_stored = forward_section(first_out, extender(first_out), sections[1])
    second_grad, second_sums = backward_section(
        second_stored, cotangent, sections[1], extender, north_weight, south_weight
    )
    first_grad, first_sums = backward_section(
        first_stored, second_grad, sections[0], extender, north_weight, south_weight
    )
    section_out = both_halves(leading, first_out, second_out, 1)[None]
    boundary_grad = both_halves(leading, first_grad, second_grad, 1)[None]
    up_part, down_part, small = reduced(chunked(first_sums), chunked(second_sums))
    up_part = up_part.T
    small = small[:, : channels // lax.axis_size(("lon", "lat"))]
    count = KERNEL * KERNEL
    stencil_part = small[:count]
    vector_part = small[count : count + 5]
    bias_count = hidden_bias.shape[1] // channels
    bias_part = small[count + 5 : count + 5 + bias_count].reshape(-1)
    return (
        section_out,
        boundary_grad,
        up_part[None],
        down_part[None],
        bias_part[None],
        stencil_part[None],
        vector_part[None],
    )


def solution(mesh):
    placed = (
        P(("groups", "lat"), "lon", None),
        P(("groups", "lat"), "lon", None),
        P("segment", None, None),
        P("segment", None),
        P("segment", None),
        P("segment", None),
        P("segment", None, None),
        P("segment", None),
        P("segment", None, None),
        P("segment", None),
        P("segment", None),
    )
    return jax.shard_map(
        local,
        mesh=mesh,
        in_specs=placed,
        out_specs=(
            P("segment", ("groups", "lat"), "lon", None),
            P("segment", ("groups", "lat"), "lon", None),
            P(("groups", "segment"), None, ("lon", "lat")),
            P(("groups", "segment"), ("lon", "lat"), None),
            P(("groups", "segment"), ("lon", "lat")),
            P(("groups", "segment"), None, ("lon", "lat")),
            P(("groups", "segment"), None, ("lon", "lat")),
        ),
        check_vma=False,
    )
```

```python
import functools
import jax
import jax.numpy as jnp
from jax import lax
from jax.experimental import pallas as pl
from jax.experimental.pallas import tpu as pltpu
from jax.sharding import PartitionSpec as P

KERNEL = 7


EPSILON = 1e-06
ROOT_HALF = 0.7071067811865476
DENSITY_SCALE = 0.3989422804014327


def extended(cells, sides, width, closed):
    for axis, dim in sides:
        count = lax.axis_size(axis)
        ends = count if closed else count - 1
        head = lax.slice_in_dim(cells, 0, width, axis=dim)
        tail = lax.slice_in_dim(cells, cells.shape[dim] - width, cells.shape[dim], axis=dim)
        cells = jnp.concatenate(
            [
                lax.ppermute(tail, axis, [(i, (i + 1) % count) for i in range(ends)]),
                cells,
                lax.ppermute(head, axis, [((i + 1) % count, i) for i in range(ends)]),
            ],
            axis=dim,
        )
    return cells


def from_behind(value, axis, steps):
    count = lax.axis_size(axis)
    pairs = [(source, (source + steps) % count) for source in range(count)]
    return lax.ppermute(value, axis, pairs)


def partner_2(shard, axis, apart):
    return lax.ppermute(shard, axis, [(i, i ^ 1 << apart) for i in range(lax.axis_size(axis))])


def correlate(padded, stencil, out_rows, out_cols):
    accumulated = jnp.zeros((out_rows, out_cols, padded.shape[2]), jnp.float32)
    for row_tap in range(KERNEL):
        for col_tap in range(KERNEL):
            window = padded[row_tap : row_tap + out_rows, col_tap : col_tap + out_cols].astype(
                jnp.float32
            )
            accumulated = accumulated + window * stencil[row_tap, col_tap].astype(jnp.float32)
    return accumulated


def edge_terms(rows, stencil, first_tap, out_cols):
    margin = rows.shape[0]
    terms = []
    for out_row in range(margin):
        total = jnp.zeros((out_cols, rows.shape[2]), jnp.float32)
        for row in range(margin):
            tap = first_tap + row - out_row
            if tap < 0 or tap >= KERNEL:
                continue
            for col_tap in range(KERNEL):
                window = rows[row, col_tap : col_tap + out_cols].astype(jnp.float32)
                total = total + window * stencil[tap, col_tap]
        terms.append(total)
    return jnp.stack(terms)


def stencil_terms(padded, grad_low, out_rows, out_cols):
    grad_wide = grad_low.astype(jnp.float32)
    columns = []
    for row_tap in range(KERNEL):
        for col_tap in range(KERNEL):
            window = padded[row_tap : row_tap + out_rows, col_tap : col_tap + out_cols].astype(
                jnp.float32
            )
            columns.append(jnp.sum(window * grad_wide, axis=(0, 1)))
    return jnp.stack(columns)


def gelu_parts(before):
    cumulative = 0.5 * (1.0 + lax.erf(before * ROOT_HALF))
    density = jnp.exp(-0.5 * before * before) * DENSITY_SCALE
    return (before * cumulative, cumulative + before * density)


def forward_section(values, padded, params):
    (
        stencil,
        conv_bias,
        norm_gain,
        norm_shift,
        up_matrix,
        bias_hidden,
        down_matrix,
        bias_out,
        scaling,
    ) = params
    out_rows, out_cols, channels = values.shape
    stencil_grid = stencil.reshape(KERNEL, KERNEL, channels)
    activity = correlate(padded, stencil_grid, out_rows, out_cols) + conv_bias
    average = jnp.mean(activity, axis=-1, keepdims=True)
    centred = activity - average
    variance = jnp.mean(centred * centred, axis=-1, keepdims=True)
    inverse = lax.rsqrt(variance + EPSILON)
    unit_norm = centred * inverse
    normed = (
        (unit_norm * norm_gain + norm_shift)
        .astype(jnp.bfloat16)
        .reshape(out_rows * out_cols, channels)
    )
    before = jnp.dot(normed, up_matrix, preferred_element_type=jnp.float32) + bias_hidden
    activated, slope_value = gelu_parts(before)
    hidden = activated.astype(jnp.bfloat16)
    branch = jnp.dot(hidden, down_matrix, preferred_element_type=jnp.float32) + bias_out
    result = (
        values.astype(jnp.float32) + scaling * branch.reshape(out_rows, out_cols, channels)
    ).astype(jnp.bfloat16)
    return (result, (padded, unit_norm, inverse, normed, slope_value, hidden, branch))


def backward_section(stored, upstream, params, extender, north_weight, south_weight):
    padded, unit_norm, inverse, normed, slope_value, hidden, branch = stored
    (
        stencil,
        conv_bias,
        norm_gain,
        norm_shift,
        up_matrix,
        bias_hidden,
        down_matrix,
        bias_out,
        scaling,
    ) = params
    out_rows, out_cols, channels = upstream.shape
    margin = KERNEL // 2
    incoming = upstream.astype(jnp.float32)
    incoming_flat = incoming.reshape(out_rows * out_cols, channels)
    scale_grad = jnp.sum(incoming_flat * branch, axis=0)
    scaled = (incoming_flat * scaling).astype(jnp.bfloat16)
    bias_out_grad = jnp.sum(scaled.astype(jnp.float32), axis=0)
    down_sum = jnp.dot(hidden.T, scaled, preferred_element_type=jnp.float32)
    hidden_grad = jnp.dot(scaled, down_matrix.T, preferred_element_type=jnp.float32)
    before_grad = (hidden_grad * slope_value).astype(jnp.bfloat16)
    up_sum = jnp.dot(before_grad.T, normed, preferred_element_type=jnp.float32)
    bias_sum = jnp.sum(before_grad.astype(jnp.float32), axis=0)
    normed_grad = jnp.dot(before_grad, up_matrix.T, preferred_element_type=jnp.float32).reshape(
        out_rows, out_cols, channels
    )
    gain_grad = jnp.sum(normed_grad * unit_norm, axis=(0, 1))
    shift_grad = jnp.sum(normed_grad, axis=(0, 1))
    gained = normed_grad * norm_gain
    activity_grad = inverse * (
        gained
        - jnp.mean(gained, axis=-1, keepdims=True)
        - unit_norm * jnp.mean(gained * unit_norm, axis=-1, keepdims=True)
    )
    activity_low = activity_grad.astype(jnp.bfloat16)
    conv_bias_grad = jnp.sum(activity_low.astype(jnp.float32), axis=(0, 1))
    stencil_sum = stencil_terms(padded, activity_low, out_rows, out_cols)
    spread = extender(activity_low)
    stencil_grid = stencil.reshape(KERNEL, KERNEL, channels).astype(jnp.float32)
    flipped = stencil_grid[::-1, ::-1]
    correction = stencil_grid[:, ::-1] - flipped
    through = correlate(spread, flipped, out_rows, out_cols)
    top_fix = edge_terms(spread[:margin], correction, 0, out_cols) * north_weight
    bottom_fix = edge_terms(spread[-margin:], correction, KERNEL - 1, out_cols) * south_weight
    rest_rows = out_rows - margin
    top_full = jnp.pad(top_fix, ((0, rest_rows), (0, 0), (0, 0)))
    bottom_full = jnp.pad(bottom_fix, ((rest_rows, 0), (0, 0), (0, 0)))
    through = through + top_full + bottom_full
    passed = (incoming + through).astype(jnp.bfloat16)
    vectors = jnp.stack([conv_bias_grad, gain_grad, shift_grad, bias_out_grad, scale_grad])
    return (passed, (up_sum, down_sum, bias_sum, stencil_sum, vectors))


def lat_neighbours(edge_rows):
    return extended(edge_rows, (("lat", 0),), KERNEL // 2, False)


CYCLE = ("lon", "segment")


def lon_neighbours(edge_cols):
    return extended(edge_cols, ((CYCLE, 1),), KERNEL // 2, True)


def pole_partner(edge_rows):
    return from_behind(edge_rows, CYCLE, lax.axis_size(CYCLE) // 2)


def hand_over(values):
    return partner_2(values, "segment", 0)


def halo_kernel(rows_ref, cols_ref, nooks_ref, rows_out, cols_out, nooks_out, send_sem, recv_sem):
    lon, lat, core = lax.axis_index("lon"), lax.axis_index("lat"), lax.axis_index("segment")
    lats, cores = lax.axis_size("lat"), lax.axis_size("segment")
    count = lax.axis_size("lon") * cores
    spot = lon * cores + core
    first = (lats - lat) // lats
    last = (lat + 1) // lats

    def device(row, column):
        column = (column + count) % count
        return {"lat": row, "lon": column // cores, "segment": column % cores}

    edges = (
        (0, lat - 1 + first, spot + first * (count // 2), 1 - first),
        (1, lat + 1 - last, spot + last * (count // 2), last),
    )
    moves = []
    for side, step in ((0, -1), (1, 1)):
        moves.append((cols_ref.at[side], cols_out.at[1 - side], side, 1 - side, lat, spot + step))
    for edge, row, column, slot in edges:
        moves.append((rows_ref.at[edge], rows_out.at[slot], 2 + edge, 2 + slot, row, column))
        for side, step in ((0, -1), (1, 1)):
            moves.append(
                (
                    nooks_ref.at[edge, side],
                    nooks_out.at[slot, 1 - side],
                    4 + 2 * edge + side,
                    4 + 2 * slot + 1 - side,
                    row,
                    column + step,
                )
            )
    barrier = pltpu.get_barrier_semaphore()
    for move in moves:
        pl.semaphore_signal(
            barrier,
            inc=1,
            device_id=device(move[4], move[5]),
            device_id_type=pl.DeviceIdType.MESH,
        )
    pl.semaphore_wait(barrier, len(moves))
    copies = [
        pltpu.make_async_remote_copy(
            src_ref=source,
            dst_ref=target,
            send_sem=send_sem.at[sent],
            recv_sem=recv_sem.at[landed],
            device_id=device(row, column),
            device_id_type=pl.DeviceIdType.MESH,
        )
        for source, target, sent, landed, row, column in moves
    ]
    for copy in copies:
        copy.start()
    for copy in copies:
        copy.wait_send()
    for index in range(2):
        for source, landed in ((cols_out, index), (rows_out, 2 + index)):
            pltpu.make_async_copy(source.at[index], source.at[index], recv_sem.at[landed]).wait()
        for side in range(2):
            spot_ref = nooks_out.at[index, side]
            pltpu.make_async_copy(spot_ref, spot_ref, recv_sem.at[4 + 2 * index + side]).wait()


def extend_local(values, northern, southern, row_source):
    margin = KERNEL // 2
    edge_rows = jnp.stack([values[:margin], values[-margin:]])
    edge_cols = jnp.stack([values[:, :margin], values[:, -margin:]])
    nooks = jnp.stack([edge_rows[:, :, :margin], edge_rows[:, :, -margin:]], axis=1)
    vmem = pl.BlockSpec(memory_space=pltpu.VMEM)
    sent = (edge_rows, edge_cols, nooks)
    rows, cols, nooks = pl.pallas_call(
        halo_kernel,
        out_shape=[jax.ShapeDtypeStruct(value.shape, value.dtype) for value in sent],
        in_specs=[vmem] * 3,
        out_specs=[vmem] * 3,
        scratch_shapes=[pltpu.SemaphoreType.DMA((8,)), pltpu.SemaphoreType.DMA((8,))],
        compiler_params=pltpu.CompilerParams(
            collective_id=1, has_side_effects=True, vmem_limit_bytes=16 * 1024 * 1024
        ),
    )(*sent)
    upper = jnp.concatenate([nooks[0, 0], rows[0], nooks[0, 1]], axis=1)
    lower = jnp.concatenate([nooks[1, 0], rows[1], nooks[1, 1]], axis=1)
    upper = jnp.where(northern, upper[::-1], upper)
    lower = jnp.where(southern, lower[::-1], lower)
    middle = jnp.concatenate([cols[0], values, cols[1]], axis=1)
    return jnp.concatenate([upper, middle, lower], axis=0)


def both_halves(leading, first, second, dim):
    received = hand_over(jnp.where(leading, second, first))
    own = jnp.where(leading, first, second)
    return jnp.where(
        leading,
        jnp.concatenate([own, received], axis=dim),
        jnp.concatenate([received, own], axis=dim),
    )


def plan(lon, lat):
    lon_bits, lat_bits = lon.bit_length() - 1, lat.bit_length() - 1
    along_lon = [("lon", bit, lon_bits - 1 - bit) for bit in range(lon_bits)]
    along_lat = [("lat", bit, lon_bits + lat_bits - 1 - bit) for bit in range(lat_bits)]
    first = along_lat + along_lon
    second = along_lon[:1] + along_lat + along_lon[1:]
    return first, second


def picked(axis, bit):
    return (slice(None),) * axis + (bit,)


def add_block(total, term, lead):
    rows = total.shape[-2]
    step = min(rows, 64)
    per = rows // step
    count = per
    for size in lead:
        count = count * size

    def body(at, carry):
        row = pl.multiple_of((at % per) * step, step)
        rest = at // per
        index = []
        for size in reversed(lead):
            index.insert(0, rest % size)
            rest = rest // size
        term(tuple(index), pl.ds(row, step))
        return carry

    lax.fori_loop(0, count, body, 0)


def reduce_kernel(orders, depth, *refs):
    parts = len(orders)
    first, second = refs[:parts], refs[parts : 2 * parts]
    outs = refs[2 * parts : 3 * parts]
    slots = [refs[3 * parts + p * (depth + 1) : 3 * parts + (p + 1) * (depth + 1)] for p in range(parts)]
    send_sem, recv_sem = refs[3 * parts + parts * (depth + 1) :]
    core = lax.axis_index("segment")
    place = {"lon": lax.axis_index("lon"), "lat": lax.axis_index("lat")}

    def bit_of(step):
        return (place[step[0]] // (1 << step[1])) % 2

    def across(step):
        own = bit_of(step)
        return {step[0]: place[step[0]] + (1 - 2 * own) * (1 << step[1])}

    barrier = pltpu.get_barrier_semaphore()
    pl.semaphore_signal(
        barrier, inc=1, device_id={"segment": 1 - core}, device_id_type=pl.DeviceIdType.MESH
    )
    for step in orders[0]:
        pl.semaphore_signal(
            barrier, inc=1, device_id=across(step), device_id_type=pl.DeviceIdType.MESH
        )
    pl.semaphore_wait(barrier, depth + 1)

    def chip_copy(part, half, source):
        step = orders[part][0]
        bit = bit_of(step)
        index = picked(step[2], 1 - bit if half == 0 else bit)
        return pltpu.make_async_remote_copy(
            src_ref=source.at[index],
            dst_ref=slots[part][0].at[index],
            send_sem=send_sem.at[part, half],
            recv_sem=recv_sem.at[part, half],
            device_id={"segment": 1 - core},
            device_id_type=pl.DeviceIdType.MESH,
        )

    def axis_copy(part, stage):
        step = orders[part][stage]
        position = step[2] - sum(1 for done in orders[part][:stage] if done[2] < step[2])
        return pltpu.make_async_remote_copy(
            src_ref=slots[part][stage].at[picked(position, 1 - bit_of(step))],
            dst_ref=slots[part][stage + 1],
            send_sem=send_sem.at[part, 2 + stage],
            recv_sem=recv_sem.at[part, 2 + stage],
            device_id=across(step),
            device_id_type=pl.DeviceIdType.MESH,
        )

    def position_of(part, stage):
        step = orders[part][stage]
        return step[2] - sum(1 for done in orders[part][:stage] if done[2] < step[2])

    def add_into(target, source, fixed_at, bit, source_at, source_bit):
        lead = target.shape[:-2]
        if fixed_at is not None:
            lead = lead[:fixed_at] + lead[fixed_at + 1 :]

        def term(index, rows):
            full = index
            if fixed_at is not None:
                full = index[:fixed_at] + (bit,) + index[fixed_at:]
            taken = full
            if source_at is not None:
                taken = full[:source_at] + (source_bit,) + full[source_at:]
            spot = full + (rows, slice(None))
            total = target[spot].astype(jnp.float32) + source[
                taken + (rows, slice(None))
            ].astype(jnp.float32)
            target[spot] = total.astype(target.dtype)

        add_block(target, term, lead)

    for half in range(2):
        for part in range(parts):

            @pl.when(core == 0)
            def _():
                chip_copy(part, half, second[part]).start()

            @pl.when(core == 1)
            def _():
                chip_copy(part, half, first[part]).start()

    for half in range(2):
        for part in range(parts):
            step = orders[part][0]
            bit = bit_of(step)
            bit = 1 - bit if half == 0 else bit
            chip_copy(part, half, first[part]).wait_recv()

            @pl.when(core == 0)
            def _():
                add_into(slots[part][0], first[part], step[2], bit, None, None)

            @pl.when(core == 1)
            def _():
                add_into(slots[part][0], second[part], step[2], bit, None, None)

            if half == 0:
                axis_copy(part, 0).start()

    for stage in range(depth):
        for part in range(parts):
            step = orders[part][stage]
            source_at, own = position_of(part, stage), bit_of(step)
            axis_copy(part, stage).wait_recv()
            source, target = slots[part][stage], slots[part][stage + 1]
            if stage + 1 < depth:
                fixed_at, bit = position_of(part, stage + 1), bit_of(orders[part][stage + 1])
                add_into(target, source, fixed_at, 1 - bit, source_at, own)
                axis_copy(part, stage + 1).start()
                add_into(target, source, fixed_at, bit, source_at, own)
            else:
                outs[part][...] = target[...].astype(jnp.float32) + source[
                    picked(source_at, own)
                ].astype(jnp.float32)
    for part in range(parts):
        for half in range(2):
            chip_copy(part, half, first[part]).wait_send()
        for stage in range(depth):
            axis_copy(part, stage).wait_send()


def reduced(first, second):
    lon, lat = lax.axis_size("lon"), lax.axis_size("lat")
    order_a, order_b = plan(lon, lat)
    orders = (order_a, order_b, order_a)
    depth = len(order_a)
    lead = (2,) * depth
    first = [value.astype(jnp.bfloat16).reshape(lead + value.shape[1:]) for value in first]
    second = [value.astype(jnp.bfloat16).reshape(lead + value.shape[1:]) for value in second]
    blocks = [value.shape[depth:] for value in first]
    scratch = [
        pltpu.VMEM((2,) * (depth - stage) + block, jnp.bfloat16)
        for block in blocks
        for stage in range(depth + 1)
    ]
    vmem = pl.BlockSpec(memory_space=pltpu.VMEM)
    return pl.pallas_call(
        functools.partial(reduce_kernel, orders, depth),
        out_shape=[jax.ShapeDtypeStruct(block, jnp.float32) for block in blocks],
        in_specs=[vmem] * (2 * len(blocks)),
        out_specs=[vmem] * len(blocks),
        scratch_shapes=scratch
        + [
            pltpu.SemaphoreType.DMA((len(blocks), depth + 2)),
            pltpu.SemaphoreType.DMA((len(blocks), depth + 2)),
        ],
        compiler_params=pltpu.CompilerParams(
            collective_id=0, has_side_effects=True, vmem_limit_bytes=48 * 1024 * 1024
        ),
    )(*first, *second)


def packed(sums):
    _, _, bias_sum, stencil_sum, vectors = sums
    channels = vectors.shape[1]
    pieces = lax.axis_size(("lon", "lat"))
    bias_rows = (
        bias_sum.reshape(pieces, -1, channels // pieces).transpose(1, 0, 2).reshape(-1, channels)
    )
    rows = jnp.concatenate([stencil_sum, vectors, bias_rows], axis=0)
    rows = rows.reshape(rows.shape[0], pieces, channels // pieces).transpose(1, 0, 2)
    return jnp.pad(rows, ((0, 0), (0, -rows.shape[1] % 16), (0, -rows.shape[2] % 128)))


def chunked(sums):
    pieces = lax.axis_size(("lon", "lat"))
    up_sum, down_sum = sums[:2]
    return (
        up_sum.reshape(pieces, -1, up_sum.shape[1]),
        down_sum.reshape(pieces, -1, down_sum.shape[1]),
        packed(sums),
    )


def local(
    inputs,
    cotangent,
    kernel,
    conv_bias,
    norm_gain,
    norm_shift,
    up_weight,
    hidden_bias,
    down_weight,
    out_bias,
    layer_scale,
):
    core = lax.axis_index("segment")
    leading = core == 0
    width = inputs.shape[1] // lax.axis_size("segment")
    channels = inputs.shape[2]
    inputs = lax.dynamic_slice_in_dim(inputs, core * width, width, axis=1)
    cotangent = lax.dynamic_slice_in_dim(cotangent, core * width, width, axis=1)
    rows = jnp.concatenate(
        [conv_bias, norm_gain, norm_shift, out_bias, layer_scale, hidden_bias.reshape(-1, channels)],
        axis=0,
    )
    taps, rows, ups, downs = [
        lax.all_gather(value, "segment", axis=0)
        for value in (kernel[0], rows, up_weight[0], down_weight[0])
    ]
    sections = [
        (
            taps[s],
            rows[s, 0],
            rows[s, 1],
            rows[s, 2],
            ups[s],
            rows[s, 5:].reshape(-1),
            downs[s],
            rows[s, 3],
            rows[s, 4],
        )
        for s in range(2)
    ]
    northern = lax.axis_index("lat") == 0
    southern = lax.axis_index("lat") == lax.axis_size("lat") - 1
    north_weight = jnp.where(northern, 1.0, 0.0).astype(jnp.float32)
    south_weight = jnp.where(southern, 1.0, 0.0).astype(jnp.float32)

    def extender(values):
        return extend_local(values, northern, southern, lat_neighbours)

    first_out, first_stored = forward_section(inputs, extender(inputs), sections[0])
    second_out, second_stored = forward_section(first_out, extender(first_out), sections[1])
    second_grad, second_sums = backward_section(
        second_stored, cotangent, sections[1], extender, north_weight, south_weight
    )
    first_grad, first_sums = backward_section(
        first_stored, second_grad, sections[0], extender, north_weight, south_weight
    )
    section_out = both_halves(leading, first_out, second_out, 1)[None]
    boundary_grad = both_halves(leading, first_grad, second_grad, 1)[None]
    up_part, down_part, small = reduced(chunked(first_sums), chunked(second_sums))
    up_part = up_part.T
    small = small[:, : channels // lax.axis_size(("lon", "lat"))]
    count = KERNEL * KERNEL
    stencil_part = small[:count]
    vector_part = small[count : count + 5]
    bias_count = hidden_bias.shape[1] // channels
    bias_part = small[count + 5 : count + 5 + bias_count].reshape(-1)
    return (
        section_out,
        boundary_grad,
        up_part[None],
        down_part[None],
        bias_part[None],
        stencil_part[None],
        vector_part[None],
    )


def solution(mesh):
    placed = (
        P(("groups", "lat"), "lon", None),
        P(("groups", "lat"), "lon", None),
        P("segment", None, None),
        P("segment", None),
        P("segment", None),
        P("segment", None),
        P("segment", None, None),
        P("segment", None),
        P("segment", None, None),
        P("segment", None),
        P("segment", None),
    )
    return jax.shard_map(
        local,
        mesh=mesh,
        in_specs=placed,
        out_specs=(
            P("segment", ("groups", "lat"), "lon", None),
            P("segment", ("groups", "lat"), "lon", None),
            P(("groups", "segment"), None, ("lon", "lat")),
            P(("groups", "segment"), ("lon", "lat"), None),
            P(("groups", "segment"), ("lon", "lat")),
            P(("groups", "segment"), None, ("lon", "lat")),
            P(("groups", "segment"), None, ("lon", "lat")),
        ),
        check_vma=False,
    )
```
